256 devices in a mesh: tower: 8 (over z), dev: 32 (over x, y, core).
Axes of the slice: x: 4, y: 4, z: 8, core: 2. Of those that a mesh axis runs over, the one named last changes fastest.
Arguments:
- grad_out: bfloat16 [8192, 8, 256], P(('tower', 'dev')), may hold values from -6 to 6
- pooled: bfloat16 [8, 32, 256, 1024], P('tower', 'dev'), may hold values from -6 to 6
- compress_w: bfloat16 [8, 1024, 256], P('tower'), may hold values from -0.1875 to 0.1875
- owner_ids: int32 [8, 32, 8192, 1], P('tower', 'dev'), may hold values from 0 to 31; in each aligned block of 8192 rows (0 to 8191, 8192 to 16383, ..., all dimensions but the last counted through in order) at most 512 rows name the same one
- slot_ids: int32 [8, 32, 8192], P('tower', 'dev'), may hold values from 0 to 1023
- touched: int32 [8, 32, 1024], P('tower', 'dev'), may hold values from 0 to 4095, as said below
- table: float32 [8, 131072, 128], P('tower', 'dev'), may hold values from -6 to 6
- accum: float32 [8, 131072], P('tower', 'dev'), may hold values from 0.05 to 2
Outputs:
- grad_compress: float32 [8, 1024, 256], P('tower', 'dev')
- new_table: float32 [8, 131072, 128], P('tower', 'dev')
- new_accum: float32 [8, 131072], P('tower', 'dev')
The draws below stay inside these ranges and needn't reach their ends.
Inputs may be any that keep to these rules, and one draw needn't show every extreme that they name: `owner_ids`: the 8192 occurrences of one device name one owner at most 512 times. `touched`: the 1024 entries of one owner are distinct rows.
All inputs are finite; a program needn't handle non-finite values.
Results may differ from the reference program's by a relative error of at most 0.0029.
Values may be sent and summed in bfloat16 or wider, within the bound.
A program may use at most 64 MiB of HBM per device.

```python
import math
import jax
import jax.numpy as jnp
import numpy as np
from jax import lax

E = 128
C = 256
HOT = 4
SAMP_DEV = 32
TOUCH = 1024
ROWS_DEV = 4096
TOWERS = 8
OWNERS = 32
GROUP = 256
K = 1024
OCC_DEV = 8192
CAP = 512
SAMPLES = 8192


def draw_touched(key, part):
    key_list = jax.random.split(key, TOWERS * OWNERS)

    def one_owner(single_key):
        shuffled = jax.random.permutation(single_key, ROWS_DEV).astype(jnp.int32)
        place_last = jnp.argmax(shuffled == ROWS_DEV - 1)
        first_row = shuffled[0]
        shuffled = shuffled.at[place_last].set(first_row).at[0].set(ROWS_DEV - 1)
        return shuffled[:TOUCH]
    return jax.vmap(one_owner)(key_list).reshape(TOWERS, OWNERS, TOUCH)


def with_ends(result, own_key, smallest, high):
    longest = result.shape.index(max(result.shape))
    spots = []
    for shift in (0, 1):
        where = [jax.random.randint(jax.random.fold_in(own_key, axis), (), 0, length) for axis, length in enumerate(result.shape)]
        where[longest] = (where[longest] + shift) % result.shape[longest]
        spots.append(tuple(where))
    return result.at[spots[0]].set(smallest).at[spots[1]].set(high)


def with_spikes(drawn, key, source, target, blocks, factor):
    owner, partner = [(jnp.arange(drawn.shape[axis_at]) // (drawn.shape[axis_at] // blocks)).reshape([-1 if axis == axis_at else 1 for axis in range(drawn.ndim)]) for axis_at in (source, target)]
    chosen = jax.random.permutation(key, blocks)[partner]
    strong = (owner == chosen) | (owner == (partner + blocks // 2) % blocks)
    return jnp.where(strong, factor * drawn, drawn)


def block_levels(stream_key, dims, cuts, smallest, largest):
    def one(axis_at, shards_of):
        draws = jax.random.uniform(jax.random.fold_in(jax.random.fold_in(stream_key, 6), axis_at), (shards_of,), jnp.float32, smallest / len(cuts), largest / len(cuts))
        return jnp.repeat(jnp.exp(draws), dims[axis_at] // shards_of).reshape((-1,) + (1,) * (len(dims) - axis_at - 1))

    loudness = one(*cuts[0])
    for cut in cuts[1:]:
        loudness = loudness * one(*cut)
    return loudness


def cumulative_ranks(count, lean):
    weights = [(1 << 20) // math.isqrt(standing ** lean) + 1 for standing in range(1, count + 1)]
    deviation = 1 + sum(weights) // (1 << 30)
    return np.cumsum(np.array([max(1, weight // deviation) for weight in weights]))


def ranked(rng, extent, count, lean):
    grid = cumulative_ranks(count, lean)
    ticket = jax.random.randint(jax.random.fold_in(rng, 1), extent, 0, int(grid[count - 1]))
    rank = jnp.searchsorted(jnp.asarray(grid, jnp.int32), ticket, side="right")
    return jax.random.permutation(jax.random.fold_in(rng, 2), count)[rank].astype(jnp.int32)


def deal_out(rng, own, number, rows, number_of, top, limit, lean):
    order = jax.random.permutation(rng, number_of)
    packed, usual = shares(number_of, rows * top, limit, lean, True), shares(number_of, rows * top, limit, lean, False)
    places = jnp.arange(number_of)

    def named(lengths, rotation):
        used = int((lengths > 0).sum())
        fixed = max(1, used // 4)
        moved = fixed + (places - fixed + rotation * (used - fixed)) % max(1, number_of - fixed)
        return jnp.zeros((number_of,), jnp.int32).at[order[jnp.where(places < fixed, places, moved)]].set(jnp.asarray(lengths, jnp.int32))

    lengths = jnp.where(number % 4 == 0, named(packed, number // 4), named(usual, number - number // 4 - 1))
    mixed = jax.random.permutation(jax.random.fold_in(own, 3), number_of)
    source_of, sink = mixed[0:number_of // 2 * 2:2], mixed[1:number_of // 2 * 2:2]
    margin = jnp.minimum(lengths[source_of] - 1, limit - lengths[sink]) // 2
    margin = jnp.where((source_of == order[0]) | (sink == order[0]) | (lengths[sink] == 0), 0, jnp.maximum(margin, 0))
    moved = jax.random.randint(jax.random.fold_in(own, 4), (number_of // 2,), 0, 1 << 20) % (margin + 1)
    lengths = lengths.at[source_of].add(-moved).at[sink].add(moved)
    members = jnp.searchsorted(jnp.cumsum(lengths), jnp.arange(rows * top), side="right").astype(jnp.int32)
    grid = members.reshape(top, rows).T
    grid = grid[jax.random.permutation(jax.random.fold_in(own, 1), rows)]
    rotation = jax.random.randint(jax.random.fold_in(own, 2), (rows, 1), 0, top)
    return jnp.take_along_axis(grid, (jnp.arange(top)[None, :] + rotation) % top, axis=1)


def shares(number_of, total, bound, slope, full):
    portions = [(1 << 20) // math.isqrt(standing ** slope) + 1 for standing in range(1, number_of + 1)]
    largest = bound if full else min(bound, max(-(-total // number_of), total * portions[0] // sum(portions)))
    least = 1 if total - largest >= number_of - 1 else 0
    holding, rest = [largest] + [least] * (number_of - 1), total - largest - least * (number_of - 1)
    while rest > 0:
        free = [i for i in range(1, number_of) if holding[i] < largest] or [i for i in range(1, number_of) if holding[i] < bound]
        mass, remaining = sum([portions[i] for i in free]), rest
        for i in free:
            extra = min(bound - holding[i], max(1, remaining * portions[i] // mass), rest)
            holding[i] = holding[i] + extra
            rest = rest - extra
    return np.array(holding)


def bell_draw(rng, dims, spread, bound, pieces=(), kind=jnp.bfloat16):
    loudness = block_levels(rng, dims, pieces, -0.22, 0.18) if pieces else 1.0
    drawn = jax.random.normal(rng, dims, jnp.float32) * spread * loudness
    return jnp.minimum(jnp.maximum(drawn, -bound), bound).astype(kind)


def bell_draw_with(own_key, extent, spread, bound, pieces, heavy, held_as=jnp.bfloat16):
    values = spread * jax.random.normal(own_key, extent, jnp.float32)
    if pieces:
        values = values * block_levels(own_key, extent, pieces, -0.22, 0.18)
    return jnp.clip(with_spikes(values, jax.random.fold_in(own_key, 3), *heavy), -bound, bound).astype(held_as)


def setup_inputs(seed: int = 0) -> dict:
    arg_keys = jax.random.split(jax.random.key(seed), 9)
    grad_out = bell_draw(arg_keys[0], (SAMPLES, TOWERS, C), 1.0, 6.0, ((0, 256),))
    pooled = bell_draw_with(arg_keys[1], (TOWERS, OWNERS, GROUP, K), 1.0, 6.0, ((0, 8), (1, 32)), (1, 3, 32, 2.75))
    compress_w = bell_draw(arg_keys[2], (TOWERS, K, C), K ** -0.5, 0.1875, ((0, 8),))
    owner_ids_keys = jax.random.split(jax.random.fold_in(arg_keys[3], 1), TOWERS * OWNERS * OCC_DEV // OCC_DEV)
    owner_ids_turns = jax.random.permutation(jax.random.fold_in(arg_keys[3], 3), TOWERS * OWNERS * OCC_DEV // OCC_DEV)
    owner_ids = jax.vmap(lambda own, number: deal_out(jax.random.fold_in(arg_keys[3], 2), own, number, OCC_DEV, OWNERS, 1, CAP, 2))(owner_ids_keys, owner_ids_turns).reshape((TOWERS, OWNERS, OCC_DEV, 1))
    slot_ids = with_ends(ranked(arg_keys[4], (TOWERS, OWNERS, OCC_DEV), TOUCH, 2), jax.random.fold_in(arg_keys[4], 3), 0, TOUCH - 1).astype(jnp.int32)
    touched = draw_touched(jax.random.fold_in(arg_keys[8], 71), 0)
    table = bell_draw(arg_keys[6], (TOWERS, OWNERS * ROWS_DEV, E), 1.0, 6.0, ((0, 8), (1, 32)), jnp.float32)
    accum = jnp.clip(jnp.exp(math.log(2.0) - 3.6888794 * jax.random.uniform(arg_keys[7], (TOWERS, OWNERS * ROWS_DEV), jnp.float32) ** block_levels(arg_keys[7], (TOWERS, OWNERS * ROWS_DEV), ((0, 8), (1, 32)), -0.2, 0.2)), 0.05, 2.0)
    return dict(grad_out=grad_out, pooled=pooled, compress_w=compress_w, owner_ids=owner_ids, slot_ids=slot_ids, touched=touched, table=table, accum=accum)


learn_rate = 0.1
epsilon = 1e-06

def one_tower(operands):
    grad_tower, pooled_rows, weight, owner_flat, slot_flat, touched_rows, table_rows, accum_rows = operands
    preact = jnp.dot(pooled_rows, weight, preferred_element_type=jnp.float32)
    sigma = jax.nn.sigmoid(preact)
    grad_pre = (grad_tower.astype(jnp.float32) * sigma * (1.0 + preact * (1.0 - sigma))).astype(jnp.bfloat16)
    grad_pooled = jnp.dot(grad_pre, weight.T, preferred_element_type=jnp.float32).astype(jnp.bfloat16)
    grad_weight = jnp.dot(pooled_rows.T, grad_pre, preferred_element_type=jnp.float32)
    bag_rows = grad_pooled.reshape(-1, E)
    occ_rows = jnp.repeat(bag_rows, HOT, axis=0).astype(jnp.float32)
    segment_ids = owner_flat * TOUCH + slot_flat
    row_grad = jax.ops.segment_sum(occ_rows, segment_ids, num_segments=OWNERS * TOUCH)
    sq_mean = lax.optimization_barrier(jnp.mean(row_grad * row_grad, axis=1))
    row_index = (jnp.arange(OWNERS, dtype=jnp.int32)[:, None] * ROWS_DEV + touched_rows).reshape(-1)
    accum_touched = accum_rows[row_index] + sq_mean
    new_accum = accum_rows.at[row_index].set(accum_touched)
    updated = table_rows[row_index] - learn_rate * row_grad / jnp.sqrt(accum_touched + epsilon)[:, None]
    new_table = table_rows.at[row_index].set(updated)
    return (grad_weight, new_table, new_accum)

def reference(grad_out, pooled, compress_w, owner_ids, slot_ids, touched, table, accum):
    grad_tower = grad_out.reshape(TOWERS, OWNERS, SAMP_DEV, TOWERS, C)
    grad_tower = grad_tower.transpose(3, 1, 0, 2, 4).reshape(TOWERS, OWNERS * GROUP, C)
    pooled_rows = pooled.reshape(TOWERS, OWNERS * GROUP, K)
    owner_flat = owner_ids.reshape(TOWERS, OWNERS * OCC_DEV)
    slot_flat = slot_ids.reshape(TOWERS, OWNERS * OCC_DEV)
    grad_compress, new_table, new_accum = lax.map(one_tower, (grad_tower, pooled_rows, compress_w, owner_flat, slot_flat, touched, table, accum))
    return (grad_compress, new_table, new_accum)
```

```python
import math

import jax
import jax.numpy as jnp
from jax import lax
from jax.experimental import pallas as pl
from jax.experimental.pallas import tpu as pltpu
from jax.sharding import PartitionSpec as P

E = 128
HOT = 4
CAP = 512


learn_rate = 0.1
epsilon = 1e-06
highest = lax.Precision.HIGHEST
f32 = jnp.float32
bf16 = jnp.bfloat16


def count_before(matches):
    row_total, length = matches.shape
    width = math.gcd(length, 128)
    blocks = length // width
    marks = matches.astype(jnp.bfloat16).reshape(row_total, blocks, width)
    lower = lax.broadcasted_iota(jnp.int32, (width, width), 0)
    upper = lax.broadcasted_iota(jnp.int32, (width, width), 1)
    inclusive = (lower <= upper).astype(jnp.bfloat16)
    within = jnp.einsum("rbi,ij->rbj", marks, inclusive, preferred_element_type=jnp.float32)
    totals = within[:, :, width - 1]
    block_a = lax.broadcasted_iota(jnp.int32, (blocks, blocks), 0)
    block_b = lax.broadcasted_iota(jnp.int32, (blocks, blocks), 1)
    strict = (block_a < block_b).astype(jnp.float32)
    offsets = jnp.dot(totals, strict, precision=highest, preferred_element_type=jnp.float32)
    ranks = within + offsets[:, :, None]
    return ranks.reshape(row_total, length).astype(jnp.int32) - 1


def accumulate(values, slot_flat, touch_count):
    total_rows = values.shape[0]
    block_size = math.gcd(total_rows, 4096)
    block_count = total_rows // block_size
    value_blocks = values.reshape(block_count, block_size, values.shape[1])
    slot_blocks = slot_flat.reshape(block_count, block_size)
    targets = lax.broadcasted_iota(jnp.int32, (touch_count, block_size), 0)

    def add_block(totals, block_pair):
        onehot = (block_pair[1][None, :] == targets).astype(jnp.bfloat16)
        return (totals + jnp.dot(onehot, block_pair[0], preferred_element_type=jnp.float32), None)

    start_sum = jnp.zeros((touch_count, values.shape[1]), jnp.float32)
    result, unused = lax.scan(add_block, start_sum, (value_blocks, slot_blocks))
    return result


def dense_pack_kernel(dest_ref, grad_ref, pooled_ref, w_ref, packed_ref, gw_ref, bag_ref, rows_ref):
    total = rows_ref.shape[0]
    step = 512

    @pl.loop(0, total // step)
    def _(i):
        rows_ref[pl.ds(pl.multiple_of(i * step, step), step), :] = jnp.zeros((step, E), f32)

    preact = jnp.dot(pooled_ref[...], w_ref[...], preferred_element_type=f32)
    sigma = 1.0 / (1.0 + jnp.exp(-preact))
    grad_pre = (grad_ref[...].astype(f32) * sigma * (1.0 + preact * (1.0 - sigma))).astype(bf16)
    gw_ref[...] = lax.dot_general(
        pooled_ref[...], grad_pre, (((0,), (0,)), ((), ())), preferred_element_type=f32
    )
    feats, group, _ = bag_ref.shape
    for f in range(feats):
        bag_ref[f] = (
            lax.dot_general(
                grad_pre,
                w_ref[f * E : (f + 1) * E, :],
                (((1,), (1,)), ((), ())),
                preferred_element_type=f32,
            )
            .astype(bf16)
            .astype(f32)
        )

    @pl.loop(0, group)
    def _(g):
        for f in range(feats):
            row = bag_ref[f, pl.ds(g, 1), :]
            for k in range(HOT):
                d = dest_ref[g * (feats * HOT) + f * HOT + k]
                rows_ref[pl.ds(d, 1), :] = row

    @pl.loop(0, total // step)
    def _(i):
        at = pl.ds(pl.multiple_of(i * step, step), step)
        packed_ref[at, :] = rows_ref[at, :].astype(bf16)


def dense_pack(dest, grad_tower, pooled_rows, weight, slot_total):
    vmem = pl.BlockSpec(memory_space=pltpu.VMEM)
    group, depth = pooled_rows.shape
    return pl.pallas_call(
        dense_pack_kernel,
        out_shape=(
            jax.ShapeDtypeStruct((slot_total, E), bf16),
            jax.ShapeDtypeStruct(weight.shape, f32),
        ),
        in_specs=[pl.BlockSpec(memory_space=pltpu.SMEM), vmem, vmem, vmem],
        out_specs=(vmem, vmem),
        scratch_shapes=[
            pltpu.VMEM((depth // E, group, E), f32),
            pltpu.VMEM((slot_total, E), f32),
        ],
        name="dense_pack",
    )(dest, grad_tower, pooled_rows, weight)


def update_kernel(rows_ref, col_ref, grad_ref, table_ref, accum_ref, out_ref, accum_out, upd_ref):
    row_grad = grad_ref[...]
    count = row_grad.shape[0]
    sq_mean = jnp.mean(row_grad * row_grad, axis=1, keepdims=True)
    col = col_ref[...]
    lanes = lax.broadcasted_iota(jnp.int32, (count, E), 1)
    blocks = accum_ref.shape[0]
    high = (lax.broadcasted_iota(jnp.int32, (count, blocks), 1) == col // E).astype(f32)
    low = (lanes == lax.rem(col, E)).astype(f32)
    spread = jnp.dot(high, accum_ref[...], precision=highest, preferred_element_type=f32)
    accum_touched = jnp.sum(spread * low, axis=1, keepdims=True) + sq_mean
    accum_out[...] = accum_ref[...] + lax.dot_general(
        high, low * sq_mean, (((0,), (0,)), ((), ())), precision=highest, preferred_element_type=f32
    )
    upd_ref[...] = learn_rate * row_grad / jnp.sqrt(accum_touched + epsilon)
    out_ref[...] = table_ref[...]

    @pl.loop(0, count // 8)
    def _(i):
        for k in range(8):
            u = i * 8 + k
            r = rows_ref[u]
            out_ref[pl.ds(r, 1), :] = table_ref[pl.ds(r, 1), :] - upd_ref[pl.ds(u, 1), :]


def update(touched, row_grad, table, accum):
    vmem = pl.BlockSpec(memory_space=pltpu.VMEM)
    new_table, new_accum = pl.pallas_call(
        update_kernel,
        out_shape=(
            jax.ShapeDtypeStruct(table.shape, f32),
            jax.ShapeDtypeStruct((accum.shape[0] // E, E), f32),
        ),
        in_specs=[pl.BlockSpec(memory_space=pltpu.SMEM), vmem, vmem, vmem, vmem],
        out_specs=(vmem, vmem),
        scratch_shapes=[pltpu.VMEM(row_grad.shape, f32)],
        name="row_update",
    )(touched, touched[:, None], row_grad, table, accum.reshape(-1, E))
    return new_table, new_accum.reshape(-1)


def shards(grad_out, pooled, compress_w, owner_ids, slot_ids, touched, table, accum):
    owners = lax.axis_size("dev")
    moved = lax.all_to_all(grad_out, "tower", split_axis=1, concat_axis=0, tiled=True)
    grad_tower = moved[:, 0, :]
    pooled_rows = pooled[0, 0]
    weight = compress_w[0]
    occurrences = owner_ids.shape[2]
    touch_count = touched.shape[2]
    slot_total = owners * CAP
    targets_own = owner_ids[0, 0, :, 0]
    slots_own = slot_ids[0, 0]
    owner_iota = lax.broadcasted_iota(jnp.int32, (owners, occurrences), 0)
    matches = targets_own[None, :] == owner_iota
    ranks = count_before(matches)
    own_rank = jnp.sum(jnp.where(matches, ranks, 0), axis=0)
    dest = targets_own * CAP + own_rank
    parts = jnp.concatenate(
        [
            jnp.where(matches, slots_own[None, :] // 32, 0).astype(bf16),
            jnp.where(matches, slots_own[None, :] % 32, 0).astype(bf16),
        ]
    )
    at_rank = (own_rank[:, None] == lax.broadcasted_iota(jnp.int32, (occurrences, CAP), 1)).astype(bf16)
    packed_slots = jnp.dot(parts, at_rank, preferred_element_type=f32)
    row_slots = (packed_slots[:owners] * 32 + packed_slots[owners:]).astype(jnp.int32)

    send_values, grad_weight = dense_pack(dest, grad_tower, pooled_rows, weight, slot_total)
    send_values = send_values.reshape(owners, CAP, E)
    recv_values, recv_slots = (
        lax.all_to_all(send_values, "dev", split_axis=0, concat_axis=0, tiled=True),
        lax.all_to_all(row_slots, "dev", split_axis=0, concat_axis=0, tiled=True),
    )
    row_grad = accumulate(recv_values.reshape(-1, E), recv_slots.reshape(-1), touch_count)
    new_table, new_accum = update(touched[0, 0], row_grad, table[0], accum[0])
    grad_weight = lax.psum_scatter(grad_weight, "dev", scatter_dimension=0, tiled=True)
    return (grad_weight[None], new_table[None], new_accum[None])


def solution(mesh):
    return jax.shard_map(
        shards,
        mesh=mesh,
        in_specs=(
            P(("tower", "dev"), None, None),
            P("tower", "dev", None, None),
            P("tower", None, None),
            P("tower", "dev", None, None),
            P("tower", "dev", None),
            P("tower", "dev", None),
            P("tower", "dev", None),
            P("tower", "dev"),
        ),
        out_specs=(P("tower", "dev", None), P("tower", "dev", None), P("tower", "dev")),
        check_vma=False,
    )
```

```python
import math

import jax
import jax.numpy as jnp
from jax import lax
from jax.experimental import pallas as pl
from jax.experimental.pallas import tpu as pltpu
from jax.sharding import PartitionSpec as P

E = 128
HOT = 4
CAP = 512


learn_rate = 0.1
epsilon = 1e-06
highest = lax.Precision.HIGHEST
MESH = pl.DeviceIdType.MESH
f32 = jnp.float32
bf16 = jnp.bfloat16


def count_before(matches):
    row_total, length = matches.shape
    width = math.gcd(length, 128)
    blocks = length // width
    marks = matches.astype(jnp.bfloat16).reshape(row_total, blocks, width)
    lower = lax.broadcasted_iota(jnp.int32, (width, width), 0)
    upper = lax.broadcasted_iota(jnp.int32, (width, width), 1)
    inclusive = (lower <= upper).astype(jnp.bfloat16)
    within = jnp.einsum("rbi,ij->rbj", marks, inclusive, preferred_element_type=jnp.float32)
    totals = within[:, :, width - 1]
    block_a = lax.broadcasted_iota(jnp.int32, (blocks, blocks), 0)
    block_b = lax.broadcasted_iota(jnp.int32, (blocks, blocks), 1)
    strict = (block_a < block_b).astype(jnp.float32)
    offsets = jnp.dot(totals, strict, precision=highest, preferred_element_type=jnp.float32)
    ranks = within + offsets[:, :, None]
    return ranks.reshape(row_total, length).astype(jnp.int32) - 1


def dense_pack_kernel(dest_ref, grad_ref, pooled_ref, w_ref, packed_ref, gw_ref, bag_ref, rows_ref):
    total = rows_ref.shape[0]
    step = 512

    @pl.loop(0, total // step)
    def _(i):
        rows_ref[pl.ds(pl.multiple_of(i * step, step), step), :] = jnp.zeros((step, E), f32)

    preact = jnp.dot(pooled_ref[...], w_ref[...], preferred_element_type=f32)
    sigma = 1.0 / (1.0 + jnp.exp(-preact))
    grad_pre = (grad_ref[...].astype(f32) * sigma * (1.0 + preact * (1.0 - sigma))).astype(bf16)
    gw_ref[...] = lax.dot_general(
        pooled_ref[...], grad_pre, (((0,), (0,)), ((), ())), preferred_element_type=f32
    )
    feats, group, _ = bag_ref.shape
    for f in range(feats):
        bag_ref[f] = (
            lax.dot_general(
                grad_pre,
                w_ref[f * E : (f + 1) * E, :],
                (((1,), (1,)), ((), ())),
                preferred_element_type=f32,
            )
            .astype(bf16)
            .astype(f32)
        )

    @pl.loop(0, group)
    def _(g):
        for f in range(feats):
            row = bag_ref[f, pl.ds(g, 1), :]
            for k in range(HOT):
                d = dest_ref[g * (feats * HOT) + f * HOT + k]
                rows_ref[pl.ds(d, 1), :] = row

    @pl.loop(0, total // step)
    def _(i):
        at = pl.ds(pl.multiple_of(i * step, step), step)
        packed_ref[at, :] = rows_ref[at, :].astype(bf16)


def dense_pack(dest, grad_tower, pooled_rows, weight, slot_total):
    vmem = pl.BlockSpec(memory_space=pltpu.VMEM)
    group, depth = pooled_rows.shape
    return pl.pallas_call(
        dense_pack_kernel,
        out_shape=(
            jax.ShapeDtypeStruct((slot_total, E), bf16),
            jax.ShapeDtypeStruct(weight.shape, f32),
        ),
        in_specs=[pl.BlockSpec(memory_space=pltpu.SMEM), vmem, vmem, vmem],
        out_specs=(vmem, vmem),
        scratch_shapes=[
            pltpu.VMEM((depth // E, group, E), f32),
            pltpu.VMEM((slot_total, E), f32),
        ],
        name="dense_pack",
    )(dest, grad_tower, pooled_rows, weight)


def update_kernel(rows_ref, col_ref, grad_ref, table_ref, accum_ref, out_ref, accum_out, upd_ref):
    row_grad = grad_ref[...]
    count = row_grad.shape[0]
    sq_mean = jnp.mean(row_grad * row_grad, axis=1, keepdims=True)
    col = col_ref[...]
    lanes = lax.broadcasted_iota(jnp.int32, (count, E), 1)
    blocks = accum_ref.shape[0]
    high = (lax.broadcasted_iota(jnp.int32, (count, blocks), 1) == col // E).astype(f32)
    low = (lanes == lax.rem(col, E)).astype(f32)
    spread = jnp.dot(high, accum_ref[...], precision=highest, preferred_element_type=f32)
    accum_touched = jnp.sum(spread * low, axis=1, keepdims=True) + sq_mean
    accum_out[...] = accum_ref[...] + lax.dot_general(
        high, low * sq_mean, (((0,), (0,)), ((), ())), precision=highest, preferred_element_type=f32
    )
    upd_ref[...] = learn_rate * row_grad / jnp.sqrt(accum_touched + epsilon)
    out_ref[...] = table_ref[...]

    @pl.loop(0, count // 8)
    def _(i):
        for k in range(8):
            u = i * 8 + k
            r = rows_ref[u]
            out_ref[pl.ds(r, 1), :] = table_ref[pl.ds(r, 1), :] - upd_ref[pl.ds(u, 1), :]


def update(touched, row_grad, table, accum):
    vmem = pl.BlockSpec(memory_space=pltpu.VMEM)
    new_table, new_accum = pl.pallas_call(
        update_kernel,
        out_shape=(
            jax.ShapeDtypeStruct(table.shape, f32),
            jax.ShapeDtypeStruct((accum.shape[0] // E, E), f32),
        ),
        in_specs=[pl.BlockSpec(memory_space=pltpu.SMEM), vmem, vmem, vmem, vmem],
        out_specs=(vmem, vmem),
        scratch_shapes=[pltpu.VMEM(row_grad.shape, f32)],
        name="row_update",
    )(touched, touched[:, None], row_grad, table, accum.reshape(-1, E))
    return new_table, new_accum.reshape(-1)


SIDE = 4
HALF = 512
GW_HALF = 16


def reduce_kernel(
    packed_ref, slots_ref, gw_ref, out_ref, gw_out,
    pk_recv, sl_recv, gw_recv, s1, r1, s2, r2, own, s3, r3, s4, r4,
    gs1, gr1, gs2, gr2, gown, gs3, gr3, gs4, gr4, send_sem, recv_sem,
):
    me = lax.axis_index("dev")
    core = lax.rem(me, 2)
    chip = me // 2
    x, y = chip // SIDE, lax.rem(chip, SIDE)
    other = 1 - core

    def device(dx, dy):
        return (lax.rem(x + dx, SIDE) * SIDE + lax.rem(y + dy, SIDE)) * 2 + core

    def owner(phase, major, minor):
        dx, dy = (major, minor) if phase == 0 else (minor, major)
        return lax.rem(x + dx, SIDE) * SIDE + lax.rem(y + dy, SIDE)

    def along_major(phase, step):
        return device(step, 0) if phase == 0 else device(0, step)

    def along_minor(phase, step):
        return along_major(1 - phase, step)

    partner = me + 1 - 2 * core
    barrier = pltpu.get_barrier_semaphore()
    for peer in (partner, device(1, 0), device(3, 0), device(0, 1), device(0, 3)):
        pl.semaphore_signal(barrier, inc=1, device_id={"dev": peer}, device_id_type=MESH)
    pl.semaphore_wait(barrier, 5)

    def remote(src, dst, number, peer):
        return pltpu.make_async_remote_copy(
            src_ref=src, dst_ref=dst, send_sem=send_sem.at[number], recv_sem=recv_sem.at[number],
            device_id={"dev": peer}, device_id_type=MESH,
        )

    slot_copy = remote(slots_ref.at[other], sl_recv, 16, partner)
    gw_copy = remote(gw_ref.at[:, other], gw_recv, 17, partner)
    slot_copy.start()
    order = [(2, dy) for dy in (0, 1, 2, 3)] + [(dx, 2) for dx in (0, 1, 3)]
    order += [(dx, dy) for dx in (1, 3, 0) for dy in (1, 3, 0)]
    pair = {}
    for number, (dx, dy) in enumerate(order):
        o = owner(0, dx, dy)
        pair[dx, dy] = remote(packed_ref.at[other, o], pk_recv.at[o], number, partner)
        pair[dx, dy].start()
    gw_copy.start()
    slot_copy.wait_recv()
    arrived = set()

    def need(phase, major, minors):
        for minor in minors:
            key = (major, minor) if phase == 0 else (minor, major)
            if key not in arrived:
                arrived.add(key)
                pair[key].wait_recv()

    def block(phase, major, minor):
        o = owner(phase, major, minor)
        ids = lax.broadcasted_iota(jnp.int32, (HALF, CAP), 0) + phase * HALF
        mine = jnp.where(slots_ref[core, o] == ids, 1.0, 0.0).astype(bf16)
        theirs = jnp.where(sl_recv[o] == ids, 1.0, 0.0).astype(bf16)
        return jnp.dot(mine, packed_ref[core, o], preferred_element_type=f32) + jnp.dot(
            theirs, pk_recv[o], preferred_element_type=f32
        )

    def gw_block(phase, major, minor):
        o = owner(phase, major, minor)
        at = pl.ds(phase * GW_HALF, GW_HALF)
        return gw_ref[o, core, at, :] + gw_recv[o, at, :]

    copies = []

    def copy1(phase, j):
        step = 1 if j < 2 else 3
        return remote(s1.at[phase, j], r1.at[phase, j], 18 + phase * 4 + j, along_major(phase, step))

    def copy2(phase, way, j):
        step = 1 if way == 0 else 3
        return remote(
            s2.at[phase, way, j], r2.at[phase, way, j], 26 + phase * 8 + way * 4 + j,
            along_major(phase, step),
        )

    def small(src, dst, number, peer):
        c = remote(src, dst, number, peer)
        copies.append(c)
        return c

    for phase in range(2):
        need(phase, 2, range(4))
        for j in range(4):
            s1[phase, j] = block(phase, 2, j).astype(bf16)
            c = copy1(phase, j)
            c.start()
            copies.append(c)

    gw_copy.wait_recv()
    g1 = {}
    for phase in range(2):
        for way in range(2):
            for j in (2 * way, 2 * way + 1):
                gs1[phase, j] = gw_block(phase, 2, j)
            at = pl.ds(2 * way, 2)
            g1[phase, way] = small(
                gs1.at[phase, at], gr1.at[phase, at], 42 + phase * 2 + way,
                along_major(phase, 1 + 2 * way),
            )
            g1[phase, way].start()

    sent2 = {}

    def second(phase, way, j, add):
        total = block(phase, 1 + 2 * way, j)
        if add:
            copies_by[phase, j].wait_recv()
            total = total + r1[phase, j].astype(f32)
        s2[phase, way, j] = total.astype(bf16)
        sent2[phase, way, j] = copy2(phase, way, j)
        sent2[phase, way, j].start()

    copies_by = {(phase, j): copies[phase * 4 + j] for phase in range(2) for j in range(4)}
    for phase in range(2):
        for way, j in ((0, 2), (1, 1), (0, 3), (1, 0)):
            need(phase, 1 + 2 * way, (j,))
            second(phase, way, j, False)
    for phase in range(2):
        for way, j in ((1, 2), (0, 1), (1, 3), (0, 0)):
            need(phase, 1 + 2 * way, (j,))
            second(phase, way, j, True)
    g2 = {}
    for phase in range(2):
        for way in range(2):
            g1[phase, way].wait_recv()
            for j in range(4):
                total = gw_block(phase, 1 + 2 * way, j)
                if j // 2 == way:
                    total = total + gr1[phase, j]
                gs2[phase, way, j] = total
            g2[phase, way] = small(
                gs2.at[phase, way], gr2.at[phase, way], 46 + phase * 2 + way,
                along_major(phase, 1 + 2 * way),
            )
            g2[phase, way].start()
    for phase in range(2):
        need(phase, 0, range(4))
        for j in range(4):
            own[phase, j] = block(phase, 0, j)
            gown[phase, j] = gw_block(phase, 0, j)

    def gathered(phase, j):
        for way in range(2):
            sent2[phase, way, j].wait_recv()
        return own[phase, j] + r2[phase, 0, j].astype(f32) + r2[phase, 1, j].astype(f32)

    sent3, sent4, g3, g4 = {}, {}, {}, {}
    quarter = HALF // 2
    for phase in range(2):
        total = gathered(phase, 2)
        for way in range(2):
            s3[phase, way] = total[way * quarter : (way + 1) * quarter].astype(bf16)
            sent3[phase, way] = small(
                s3.at[phase, way], r3.at[phase, way], 50 + phase * 2 + way,
                along_minor(phase, 1 + 2 * way),
            )
            sent3[phase, way].start()
    for phase in range(2):
        for way in range(2):
            g2[phase, way].wait_recv()
        for j in range(4):
            gown[phase, j] = gown[phase, j] + gr2[phase, 0, j] + gr2[phase, 1, j]
        for way in range(2):
            gs3[phase, way] = gown[phase, 2, 8 * way : 8 * way + 8]
            g3[phase, way] = small(
                gs3.at[phase, way], gr3.at[phase, way], 54 + phase * 2 + way,
                along_minor(phase, 1 + 2 * way),
            )
            g3[phase, way].start()
    for phase in range(2):
        for way in range(2):
            total = gathered(phase, 1 + 2 * way)
            sent3[phase, way].wait_recv()
            for part in range(2):
                at = slice(part * quarter, (part + 1) * quarter)
                piece = total[at]
                if part == way:
                    piece = piece + r3[phase, way].astype(f32)
                s4[phase, way, at] = piece.astype(bf16)
            sent4[phase, way] = small(
                s4.at[phase, way], r4.at[phase, way], 58 + phase * 2 + way,
                along_minor(phase, 1 + 2 * way),
            )
            sent4[phase, way].start()
            g3[phase, way].wait_recv()
            for part in range(2):
                at = slice(8 * part, 8 * part + 8)
                piece = gown[phase, 1 + 2 * way, at]
                if part == way:
                    piece = piece + gr3[phase, way]
                gs4[phase, way, at] = piece
            g4[phase, way] = small(
                gs4.at[phase, way], gr4.at[phase, way], 62 + phase * 2 + way,
                along_minor(phase, 1 + 2 * way),
            )
            g4[phase, way].start()
    for phase in range(2):
        own[phase, 0] = gathered(phase, 0)
    for phase in range(2):
        for way in range(2):
            sent4[phase, way].wait_recv()
            g4[phase, way].wait_recv()
        out_ref[pl.ds(phase * HALF, HALF), :] = (
            own[phase, 0] + r4[phase, 0].astype(f32) + r4[phase, 1].astype(f32)
        )
        gw_out[pl.ds(phase * GW_HALF, GW_HALF), :] = gown[phase, 0] + gr4[phase, 0] + gr4[phase, 1]
    for c in [slot_copy, gw_copy, *pair.values(), *copies, *sent2.values()]:
        c.wait_send()


def reduce_rows(packed, slots, grad_weight):
    vmem = pl.BlockSpec(memory_space=pltpu.VMEM)
    cols = grad_weight.shape[-1]
    halves = (HALF, E)
    small = (GW_HALF, cols)
    return pl.pallas_call(
        reduce_kernel,
        out_shape=(
            jax.ShapeDtypeStruct((2 * HALF, E), f32),
            jax.ShapeDtypeStruct((2 * GW_HALF, cols), f32),
        ),
        in_specs=[vmem, vmem, vmem],
        out_specs=(vmem, vmem),
        scratch_shapes=[
            pltpu.VMEM((16, CAP, E), bf16),
            pltpu.VMEM((16, 1, CAP), jnp.int32),
            pltpu.VMEM((16, 2 * GW_HALF, cols), f32),
            pltpu.VMEM((2, 4, *halves), bf16),
            pltpu.VMEM((2, 4, *halves), bf16),
            pltpu.VMEM((2, 2, 4, *halves), bf16),
            pltpu.VMEM((2, 2, 4, *halves), bf16),
            pltpu.VMEM((2, 4, *halves), f32),
            pltpu.VMEM((2, 2, HALF // 2, E), bf16),
            pltpu.VMEM((2, 2, HALF // 2, E), bf16),
            pltpu.VMEM((2, 2, *halves), bf16),
            pltpu.VMEM((2, 2, *halves), bf16),
            pltpu.VMEM((2, 4, *small), f32),
            pltpu.VMEM((2, 4, *small), f32),
            pltpu.VMEM((2, 2, 4, *small), f32),
            pltpu.VMEM((2, 2, 4, *small), f32),
            pltpu.VMEM((2, 4, *small), f32),
            pltpu.VMEM((2, 2, GW_HALF // 2, cols), f32),
            pltpu.VMEM((2, 2, GW_HALF // 2, cols), f32),
            pltpu.VMEM((2, 2, *small), f32),
            pltpu.VMEM((2, 2, *small), f32),
            pltpu.SemaphoreType.DMA((66,)),
            pltpu.SemaphoreType.DMA((66,)),
        ],
        compiler_params=pltpu.CompilerParams(collective_id=0, has_side_effects=True),
        name="reduce_rows",
    )(packed, slots, grad_weight)


def shards(grad_out, pooled, compress_w, owner_ids, slot_ids, touched, table, accum):
    owners = lax.axis_size("dev")
    moved = lax.all_to_all(grad_out, "tower", split_axis=1, concat_axis=0, tiled=True)
    grad_tower = moved[:, 0, :]
    pooled_rows = pooled[0, 0]
    weight = compress_w[0]
    occurrences = owner_ids.shape[2]
    slot_total = owners * CAP
    owner_own = owner_ids[0, 0, :, 0]
    targets_own = (owner_own % 2) * (owners // 2) + owner_own // 2
    slots_own = slot_ids[0, 0]
    owner_iota = lax.broadcasted_iota(jnp.int32, (owners, occurrences), 0)
    matches = targets_own[None, :] == owner_iota
    ranks = count_before(matches)
    own_rank = jnp.sum(jnp.where(matches, ranks, 0), axis=0)
    dest = targets_own * CAP + own_rank
    parts = jnp.concatenate(
        [
            jnp.where(matches, slots_own[None, :] // 32, 0).astype(bf16),
            jnp.where(matches, slots_own[None, :] % 32, 0).astype(bf16),
        ]
    )
    at_rank = (own_rank[:, None] == lax.broadcasted_iota(jnp.int32, (occurrences, CAP), 1)).astype(bf16)
    packed_slots = jnp.dot(parts, at_rank, preferred_element_type=f32)
    row_slots = (packed_slots[:owners] * 32 + packed_slots[owners:]).astype(jnp.int32)

    packed, grad_weight = dense_pack(dest, grad_tower, pooled_rows, weight, slot_total)
    chips = owners // 2
    row_grad, grad_weight = reduce_rows(
        packed.reshape(2, chips, CAP, E),
        row_slots.reshape(2, chips, 1, CAP),
        grad_weight.reshape(chips, 2, -1, grad_weight.shape[1]),
    )
    new_table, new_accum = update(touched[0, 0], row_grad, table[0], accum[0])
    return (grad_weight[None], new_table[None], new_accum[None])


def solution(mesh):
    return jax.shard_map(
        shards,
        mesh=mesh,
        in_specs=(
            P(("tower", "dev"), None, None),
            P("tower", "dev", None, None),
            P("tower", None, None),
            P("tower", "dev", None, None),
            P("tower", "dev", None),
            P("tower", "dev", None),
            P("tower", "dev", None),
            P("tower", "dev"),
        ),
        out_specs=(P("tower", "dev", None), P("tower", "dev", None), P("tower", "dev")),
        check_vma=False,
    )
```

```python
import jax
import jax.numpy as jnp
from jax import lax
from jax.experimental import pallas as pl
from jax.experimental.pallas import tpu as pltpu
from jax.sharding import PartitionSpec as P

E = 128
HOT = 4
CAP = 512
FEATS = 8
OWNERS = 32


learn_rate = 0.1
epsilon = 1e-06
highest = lax.Precision.HIGHEST
MESH = pl.DeviceIdType.MESH
f32 = jnp.float32
bf16 = jnp.bfloat16


def front_kernel(
    grad_ref, pooled_ref, w_ref, owner_ref, slot_ref, bags_ref, gw_ref, dest_ref, slots_ref,
    sbuf, rbuf, marks_ref, count_ref, rank_ref, list_ref, send_sem, recv_sem,
):
    me = lax.axis_index("tower")
    towers = grad_ref.shape[1]
    barrier = pltpu.get_barrier_semaphore()
    for k in range(1, towers):
        pl.semaphore_signal(
            barrier, inc=1, device_id={"tower": lax.rem(me + k, towers)}, device_id_type=MESH
        )
    sent = grad_ref[...].astype(f32)
    for t in range(towers):
        sbuf[t] = sent[:, t, :].astype(bf16)
    pl.semaphore_wait(barrier, towers - 1)
    copies = []
    for k in sorted(range(1, towers), key=lambda k: -min(k, towers - k)):
        peer = lax.rem(me + k, towers)
        c = pltpu.make_async_remote_copy(
            src_ref=sbuf.at[peer], dst_ref=rbuf.at[me], send_sem=send_sem.at[k],
            recv_sem=recv_sem.at[k], device_id={"tower": peer}, device_id_type=MESH,
        )
        c.start()
        copies.append(c)
    rbuf[me] = sbuf[me]

    blocks = owner_ref.shape[0]
    sub = lax.broadcasted_iota(jnp.int32, (OWNERS, E), 0)
    owner = owner_ref[...]
    target = (owner & 1) * (OWNERS // 2) + (owner >> 1)
    for b in range(blocks):
        marks_ref[b * OWNERS : (b + 1) * OWNERS, :] = jnp.where(
            target[b : b + 1, :] == sub, 1.0, 0.0
        ).astype(bf16)
    row = lax.broadcasted_iota(jnp.int32, (E, 2 * E), 0)
    col = lax.broadcasted_iota(jnp.int32, (E, 2 * E), 1)
    before = jnp.where(row <= col, 1.0, 0.0).astype(bf16)
    count_ref[...] = jnp.dot(marks_ref[...], before, preferred_element_type=f32)
    run = jnp.zeros((OWNERS, E), f32)
    for b in range(blocks):
        at = slice(b * OWNERS, (b + 1) * OWNERS)
        mark = marks_ref[at, :].astype(f32)
        rank = jnp.sum(mark * (count_ref[at, :E] + run), axis=0, keepdims=True)
        rank_ref[b : b + 1, :] = rank.astype(jnp.int32) - 1
        run = run + count_ref[at, E:]
    dest_ref[...] = target * CAP + rank_ref[...]

    list_ref[...] = jnp.zeros(list_ref.shape, f32)
    step = 8

    @pl.loop(0, blocks // step)
    def _(c):
        at = pl.ds(pl.multiple_of(c * step, step), step)
        ranks = rank_ref[at, :]
        slots = slot_ref[at, :]
        high = (slots >> 5).astype(f32)
        low = (slots & 31).astype(f32)
        ids = lax.broadcasted_iota(jnp.int32, (CAP, E), 0)
        at_rank, parts = [], []
        for j in range(step):
            one = slice(j, j + 1)
            at_rank.append(jnp.where(ranks[one] == ids, 1.0, 0.0).astype(bf16))
            base = pl.multiple_of(c * (step * OWNERS) + j * OWNERS, OWNERS)
            mark = marks_ref[pl.ds(base, OWNERS), :].astype(f32)
            parts.append(
                jnp.concatenate([mark * high[one], mark * low[one]], axis=0).astype(bf16)
            )
        list_ref[...] += lax.dot_general(
            jnp.concatenate(parts, axis=1), jnp.concatenate(at_rank, axis=1),
            (((1,), (1,)), ((), ())), preferred_element_type=f32,
        )

    slots_ref[...] = (list_ref[:OWNERS] * 32.0 + list_ref[OWNERS:]).astype(jnp.int32)

    preact = jnp.dot(pooled_ref[...], w_ref[...], preferred_element_type=f32)
    sigma = 1.0 / (1.0 + jnp.exp(-preact))
    for c in copies:
        c.wait_recv()
    moved = rbuf[...].reshape(preact.shape)
    grad_pre = (moved.astype(f32) * sigma * (1.0 + preact * (1.0 - sigma))).astype(bf16)
    gw_ref[...] = lax.dot_general(
        pooled_ref[...], grad_pre, (((0,), (0,)), ((), ())), preferred_element_type=f32
    )
    group = preact.shape[0]
    for f in range(w_ref.shape[0] // E):
        bags_ref[f * group : (f + 1) * group, :] = (
            lax.dot_general(
                grad_pre, w_ref[f * E : (f + 1) * E, :], (((1,), (1,)), ((), ())),
                preferred_element_type=f32,
            )
            .astype(bf16)
            .astype(f32)
        )
    for c in copies:
        c.wait_send()


def front(grad_out, pooled_rows, weight, owner_rows, slot_rows):
    vmem = pl.BlockSpec(memory_space=pltpu.VMEM)
    samples, towers, cols = grad_out.shape
    group, depth = pooled_rows.shape
    blocks = owner_rows.shape[0]
    return pl.pallas_call(
        front_kernel,
        out_shape=(
            jax.ShapeDtypeStruct((depth // E * group, E), f32),
            jax.ShapeDtypeStruct(weight.shape, f32),
            jax.ShapeDtypeStruct(owner_rows.shape, jnp.int32),
            jax.ShapeDtypeStruct((OWNERS, CAP), jnp.int32),
        ),
        in_specs=[vmem] * 5,
        out_specs=(vmem,) * 4,
        scratch_shapes=[
            pltpu.VMEM((towers, samples, cols), bf16),
            pltpu.VMEM((towers, samples, cols), bf16),
            pltpu.VMEM((blocks * OWNERS, E), bf16),
            pltpu.VMEM((blocks * OWNERS, 2 * E), f32),
            pltpu.VMEM((blocks, E), jnp.int32),
            pltpu.VMEM((2 * OWNERS, CAP), f32),
            pltpu.SemaphoreType.DMA((towers,)),
            pltpu.SemaphoreType.DMA((towers,)),
        ],
        compiler_params=pltpu.CompilerParams(collective_id=1, has_side_effects=True),
        name="front",
    )(grad_out, pooled_rows, weight, owner_rows, slot_rows)


def pack_kernel(dest_ref, bag_ref, packed_ref, rows_ref):
    total = rows_ref.shape[0]
    step = 512

    @pl.loop(0, total // step)
    def _(i):
        rows_ref[pl.ds(pl.multiple_of(i * step, step), step), :] = jnp.zeros((step, E), f32)

    group = bag_ref.shape[0] // FEATS

    @pl.loop(0, group // 2)
    def _(i):
        for g in (2 * i, 2 * i + 1):
            for f in range(FEATS):
                row = bag_ref[pl.ds(f * group + g, 1), :]
                for k in range(HOT):
                    d = dest_ref[g * (FEATS * HOT) + f * HOT + k]
                    rows_ref[pl.ds(d, 1), :] = row

    @pl.loop(0, total // step)
    def _(i):
        at = pl.ds(pl.multiple_of(i * step, step), step)
        packed_ref[at, :] = rows_ref[at, :].astype(bf16)


def pack(dest, bags, slot_total):
    vmem = pl.BlockSpec(memory_space=pltpu.VMEM)
    return pl.pallas_call(
        pack_kernel,
        out_shape=jax.ShapeDtypeStruct((slot_total, E), bf16),
        in_specs=[pl.BlockSpec(memory_space=pltpu.SMEM), vmem],
        out_specs=vmem,
        scratch_shapes=[pltpu.VMEM((slot_total, E), f32)],
        name="pack",
    )(dest, bags)


def update_kernel(
    rows_ref, lane_ref, grad_ref, table_ref, accum_ref, gw_ref, out_ref, accum_out, gw_out, upd_ref
):
    gw_out[...] = gw_ref[...]
    row_grad = grad_ref[...]
    count = row_grad.shape[0]
    sq_mean = jnp.mean(row_grad * row_grad, axis=1, keepdims=True)
    col = jnp.concatenate(
        [
            jnp.broadcast_to(lane_ref[b : b + 1, :].astype(f32), (E, E)).T
            for b in range(count // E)
        ]
    ).astype(jnp.int32)
    lanes = lax.broadcasted_iota(jnp.int32, (count, E), 1)
    blocks = accum_ref.shape[0]
    high = ((col >> 7) == lanes).astype(f32)[:, :blocks]
    low = ((col & 127) == lanes).astype(f32)
    spread = jnp.dot(high, accum_ref[...], precision=highest, preferred_element_type=f32)
    accum_touched = jnp.sum(spread * low, axis=1, keepdims=True) + sq_mean
    accum_out[...] = accum_ref[...] + lax.dot_general(
        high, low * sq_mean, (((0,), (0,)), ((), ())), precision=highest, preferred_element_type=f32
    )
    upd_ref[...] = learn_rate * row_grad / jnp.sqrt(accum_touched + epsilon)
    out_ref[...] = table_ref[...]

    @pl.loop(0, count // 16)
    def _(i):
        for k in range(16):
            u = i * 16 + k
            r = rows_ref[u]
            out_ref[pl.ds(r, 1), :] = table_ref[pl.ds(r, 1), :] - upd_ref[pl.ds(u, 1), :]


def update(touched, row_grad, table, accum, grad_weight):
    vmem = pl.BlockSpec(memory_space=pltpu.VMEM)
    new_table, new_accum, grad_weight = pl.pallas_call(
        update_kernel,
        out_shape=(
            jax.ShapeDtypeStruct(table.shape, f32),
            jax.ShapeDtypeStruct((accum.shape[0] // E, E), f32),
            jax.ShapeDtypeStruct(grad_weight.shape, f32),
        ),
        in_specs=[pl.BlockSpec(memory_space=pltpu.SMEM), vmem, vmem, vmem, vmem, vmem],
        out_specs=(vmem, vmem, vmem),
        scratch_shapes=[pltpu.VMEM(row_grad.shape, f32)],
        name="row_update",
    )(touched, touched.reshape(-1, E), row_grad, table, accum.reshape(-1, E), grad_weight)
    return new_table, new_accum.reshape(-1), grad_weight


SIDE = 4
HALF = 512
GW_HALF = 16


def reduce_kernel(
    packed_ref, slots_ref, gw_ref, out_ref, gw_out,
    pk_recv, sl_recv, gw_recv, s1, r1, s2, r2, own, s3, r3, s4, r4,
    gs1, gr1, gs2, gr2, gown, gs3, gr3, gs4, gr4, send_sem, recv_sem,
):
    me = lax.axis_index("dev")
    core = lax.rem(me, 2)
    chip = me // 2
    x, y = chip // SIDE, lax.rem(chip, SIDE)
    other = 1 - core

    def device(dx, dy):
        return (lax.rem(x + dx, SIDE) * SIDE + lax.rem(y + dy, SIDE)) * 2 + core

    def owner(phase, major, minor):
        dx, dy = (major, minor) if phase == 0 else (minor, major)
        return lax.rem(x + dx, SIDE) * SIDE + lax.rem(y + dy, SIDE)

    def along_major(phase, step):
        return device(step, 0) if phase == 0 else device(0, step)

    def along_minor(phase, step):
        return along_major(1 - phase, step)

    partner = me + 1 - 2 * core
    barrier = pltpu.get_barrier_semaphore()
    for peer in (partner, device(1, 0), device(3, 0), device(0, 1), device(0, 3)):
        pl.semaphore_signal(barrier, inc=1, device_id={"dev": peer}, device_id_type=MESH)
    pl.semaphore_wait(barrier, 5)

    def remote(src, dst, number, peer):
        return pltpu.make_async_remote_copy(
            src_ref=src, dst_ref=dst, send_sem=send_sem.at[number], recv_sem=recv_sem.at[number],
            device_id={"dev": peer}, device_id_type=MESH,
        )

    slot_copy = remote(slots_ref.at[other], sl_recv, 16, partner)
    gw_copy = remote(gw_ref.at[:, other], gw_recv, 17, partner)
    slot_copy.start()
    order = [(2, dy) for dy in (0, 1, 2, 3)] + [(dx, 2) for dx in (0, 1, 3)]
    order += [(dx, dy) for dx in (1, 3, 0) for dy in (1, 3, 0)]
    pair = {}
    for number, (dx, dy) in enumerate(order):
        o = owner(0, dx, dy)
        pair[dx, dy] = remote(packed_ref.at[other, o], pk_recv.at[o], number, partner)
        pair[dx, dy].start()
    gw_copy.start()
    slot_copy.wait_recv()
    arrived = set()

    def need(phase, major, minors):
        for minor in minors:
            key = (major, minor) if phase == 0 else (minor, major)
            if key not in arrived:
                arrived.add(key)
                pair[key].wait_recv()

    def block(phase, major, minor):
        o = owner(phase, major, minor)
        ids = lax.broadcasted_iota(jnp.int32, (HALF, CAP), 0) + phase * HALF
        mine = jnp.where(slots_ref[core, o] == ids, 1.0, 0.0).astype(bf16)
        theirs = jnp.where(sl_recv[o] == ids, 1.0, 0.0).astype(bf16)
        return jnp.dot(mine, packed_ref[core, o], preferred_element_type=f32) + jnp.dot(
            theirs, pk_recv[o], preferred_element_type=f32
        )

    def gw_block(phase, major, minor):
        o = owner(phase, major, minor)
        at = pl.ds(phase * GW_HALF, GW_HALF)
        return gw_ref[o, core, at, :] + gw_recv[o, at, :]

    copies = []

    def copy1(phase, j):
        step = 1 if j < 2 else 3
        return remote(s1.at[phase, j], r1.at[phase, j], 18 + phase * 4 + j, along_major(phase, step))

    def copy2(phase, way, j):
        step = 1 if way == 0 else 3
        return remote(
            s2.at[phase, way, j], r2.at[phase, way, j], 26 + phase * 8 + way * 4 + j,
            along_major(phase, step),
        )

    def small(src, dst, number, peer):
        c = remote(src, dst, number, peer)
        copies.append(c)
        return c

    for phase in range(2):
        need(phase, 2, range(4))
        for j in range(4):
            s1[phase, j] = block(phase, 2, j).astype(bf16)
            c = copy1(phase, j)
            c.start()
            copies.append(c)

    gw_copy.wait_recv()
    g1 = {}
    for phase in range(2):
        for way in range(2):
            for j in (2 * way, 2 * way + 1):
                gs1[phase, j] = gw_block(phase, 2, j)
            at = pl.ds(2 * way, 2)
            g1[phase, way] = small(
                gs1.at[phase, at], gr1.at[phase, at], 42 + phase * 2 + way,
                along_major(phase, 1 + 2 * way),
            )
            g1[phase, way].start()

    sent2 = {}

    def second(phase, way, j, add):
        total = block(phase, 1 + 2 * way, j)
        if add:
            copies_by[phase, j].wait_recv()
            total = total + r1[phase, j].astype(f32)
        s2[phase, way, j] = total.astype(bf16)
        sent2[phase, way, j] = copy2(phase, way, j)
        sent2[phase, way, j].start()

    copies_by = {(phase, j): copies[phase * 4 + j] for phase in range(2) for j in range(4)}
    for phase in range(2):
        for way, j in ((0, 2), (1, 1), (0, 3), (1, 0)):
            need(phase, 1 + 2 * way, (j,))
            second(phase, way, j, False)
    for phase in range(2):
        for way, j in ((1, 2), (0, 1), (1, 3), (0, 0)):
            need(phase, 1 + 2 * way, (j,))
            second(phase, way, j, True)
    g2 = {}
    for phase in range(2):
        for way in range(2):
            g1[phase, way].wait_recv()
            for j in range(4):
                total = gw_block(phase, 1 + 2 * way, j)
                if j // 2 == way:
                    total = total + gr1[phase, j]
                gs2[phase, way, j] = total
            g2[phase, way] = small(
                gs2.at[phase, way], gr2.at[phase, way], 46 + phase * 2 + way,
                along_major(phase, 1 + 2 * way),
            )
            g2[phase, way].start()
    for phase in range(2):
        need(phase, 0, range(4))
        for j in range(4):
            own[phase, j] = block(phase, 0, j)
            gown[phase, j] = gw_block(phase, 0, j)

    def gathered(phase, j):
        for way in range(2):
            sent2[phase, way, j].wait_recv()
        return own[phase, j] + r2[phase, 0, j].astype(f32) + r2[phase, 1, j].astype(f32)

    sent3, sent4, g3, g4 = {}, {}, {}, {}
    quarter = HALF // 2
    for phase in range(2):
        total = gathered(phase, 2)
        for way in range(2):
            s3[phase, way] = total[way * quarter : (way + 1) * quarter].astype(bf16)
            sent3[phase, way] = small(
                s3.at[phase, way], r3.at[phase, way], 50 + phase * 2 + way,
                along_minor(phase, 1 + 2 * way),
            )
            sent3[phase, way].start()
    for phase in range(2):
        for way in range(2):
            g2[phase, way].wait_recv()
        for j in range(4):
            gown[phase, j] = gown[phase, j] + gr2[phase, 0, j] + gr2[phase, 1, j]
        for way in range(2):
            gs3[phase, way] = gown[phase, 2, 8 * way : 8 * way + 8]
            g3[phase, way] = small(
                gs3.at[phase, way], gr3.at[phase, way], 54 + phase * 2 + way,
                along_minor(phase, 1 + 2 * way),
            )
            g3[phase, way].start()
    for phase in range(2):
        for way in range(2):
            total = gathered(phase, 1 + 2 * way)
            sent3[phase, way].wait_recv()
            for part in range(2):
                at = slice(part * quarter, (part + 1) * quarter)
                piece = total[at]
                if part == way:
                    piece = piece + r3[phase, way].astype(f32)
                s4[phase, way, at] = piece.astype(bf16)
            sent4[phase, way] = small(
                s4.at[phase, way], r4.at[phase, way], 58 + phase * 2 + way,
                along_minor(phase, 1 + 2 * way),
            )
            sent4[phase, way].start()
            g3[phase, way].wait_recv()
            for part in range(2):
                at = slice(8 * part, 8 * part + 8)
                piece = gown[phase, 1 + 2 * way, at]
                if part == way:
                    piece = piece + gr3[phase, way]
                gs4[phase, way, at] = piece
            g4[phase, way] = small(
                gs4.at[phase, way], gr4.at[phase, way], 62 + phase * 2 + way,
                along_minor(phase, 1 + 2 * way),
            )
            g4[phase, way].start()
    for phase in range(2):
        own[phase, 0] = gathered(phase, 0)
    for phase in range(2):
        for way in range(2):
            sent4[phase, way].wait_recv()
            g4[phase, way].wait_recv()
        out_ref[pl.ds(phase * HALF, HALF), :] = (
            own[phase, 0] + r4[phase, 0].astype(f32) + r4[phase, 1].astype(f32)
        )
        gw_out[pl.ds(phase * GW_HALF, GW_HALF), :] = gown[phase, 0] + gr4[phase, 0] + gr4[phase, 1]
    for c in [slot_copy, gw_copy, *pair.values(), *copies, *sent2.values()]:
        c.wait_send()


def reduce_rows(packed, slots, grad_weight):
    vmem = pl.BlockSpec(memory_space=pltpu.VMEM)
    cols = grad_weight.shape[-1]
    halves = (HALF, E)
    small = (GW_HALF, cols)
    return pl.pallas_call(
        reduce_kernel,
        out_shape=(
            jax.ShapeDtypeStruct((2 * HALF, E), f32),
            jax.ShapeDtypeStruct((2 * GW_HALF, cols), f32),
        ),
        in_specs=[vmem, vmem, vmem],
        out_specs=(vmem, vmem),
        scratch_shapes=[
            pltpu.VMEM((16, CAP, E), bf16),
            pltpu.VMEM((16, 1, CAP), jnp.int32),
            pltpu.VMEM((16, 2 * GW_HALF, cols), f32),
            pltpu.VMEM((2, 4, *halves), bf16),
            pltpu.VMEM((2, 4, *halves), bf16),
            pltpu.VMEM((2, 2, 4, *halves), bf16),
            pltpu.VMEM((2, 2, 4, *halves), bf16),
            pltpu.VMEM((2, 4, *halves), f32),
            pltpu.VMEM((2, 2, HALF // 2, E), bf16),
            pltpu.VMEM((2, 2, HALF // 2, E), bf16),
            pltpu.VMEM((2, 2, *halves), bf16),
            pltpu.VMEM((2, 2, *halves), bf16),
            pltpu.VMEM((2, 4, *small), f32),
            pltpu.VMEM((2, 4, *small), f32),
            pltpu.VMEM((2, 2, 4, *small), f32),
            pltpu.VMEM((2, 2, 4, *small), f32),
            pltpu.VMEM((2, 4, *small), f32),
            pltpu.VMEM((2, 2, GW_HALF // 2, cols), f32),
            pltpu.VMEM((2, 2, GW_HALF // 2, cols), f32),
            pltpu.VMEM((2, 2, *small), f32),
            pltpu.VMEM((2, 2, *small), f32),
            pltpu.SemaphoreType.DMA((66,)),
            pltpu.SemaphoreType.DMA((66,)),
        ],
        compiler_params=pltpu.CompilerParams(collective_id=0, has_side_effects=True),
        name="reduce_rows",
    )(packed, slots, grad_weight)


def shards(grad_out, pooled, compress_w, owner_ids, slot_ids, touched, table, accum):
    chips = OWNERS // 2
    bags, grad_weight, dest, slots = front(
        grad_out,
        pooled[0, 0],
        compress_w[0],
        owner_ids.reshape(-1, E),
        slot_ids.reshape(-1, E),
    )
    packed = pack(dest.reshape(-1), bags, OWNERS * CAP)
    row_grad, grad_weight = reduce_rows(
        packed.reshape(2, chips, CAP, E),
        slots.reshape(2, chips, 1, CAP),
        grad_weight.reshape(chips, 2, -1, grad_weight.shape[1]),
    )
    new_table, new_accum, grad_weight = update(
        touched[0, 0], row_grad, table[0], accum[0], grad_weight
    )
    return (grad_weight[None], new_table[None], new_accum[None])


def solution(mesh):
    return jax.shard_map(
        shards,
        mesh=mesh,
        in_specs=(
            P(("tower", "dev"), None, None),
            P("tower", "dev", None, None),
            P("tower", None, None),
            P("tower", "dev", None, None),
            P("tower", "dev", None),
            P("tower", "dev", None),
            P("tower", "dev", None),
            P("tower", "dev"),
        ),
        out_specs=(P("tower", "dev", None), P("tower", "dev", None), P("tower", "dev")),
        check_vma=False,
    )
```

```python
import jax
import jax.numpy as jnp
from jax import lax
from jax.experimental import pallas as pl
from jax.experimental.pallas import tpu as pltpu
from jax.sharding import PartitionSpec as P

E = 128
HOT = 4
CAP = 512
FEATS = 8
OWNERS = 32


learn_rate = 0.1
epsilon = 1e-06
highest = lax.Precision.HIGHEST
MESH = pl.DeviceIdType.MESH
f32 = jnp.float32
bf16 = jnp.bfloat16


def front_kernel(
    grad_ref, pooled_ref, w_ref, owner_ref, slot_ref, bags_ref, gw_ref, from_ref, slots_ref,
    sbuf, rbuf, marks_ref, count_ref, rank_ref, list_ref, send_sem, recv_sem,
):
    me = lax.axis_index("tower")
    towers = grad_ref.shape[1]
    barrier = pltpu.get_barrier_semaphore()
    for k in range(1, towers):
        pl.semaphore_signal(
            barrier, inc=1, device_id={"tower": lax.rem(me + k, towers)}, device_id_type=MESH
        )
    sent = grad_ref[...].astype(f32)
    for t in range(towers):
        sbuf[t] = sent[:, t, :].astype(bf16)
    pl.semaphore_wait(barrier, towers - 1)
    copies = []
    for k in sorted(range(1, towers), key=lambda k: -min(k, towers - k)):
        peer = lax.rem(me + k, towers)
        c = pltpu.make_async_remote_copy(
            src_ref=sbuf.at[peer], dst_ref=rbuf.at[me], send_sem=send_sem.at[k],
            recv_sem=recv_sem.at[k], device_id={"tower": peer}, device_id_type=MESH,
        )
        c.start()
        copies.append(c)
    rbuf[me] = sbuf[me]

    blocks = owner_ref.shape[0]
    sub = lax.broadcasted_iota(jnp.int32, (OWNERS, E), 0)
    owner = owner_ref[...]
    target = (owner & 1) * (OWNERS // 2) + (owner >> 1)
    for b in range(blocks):
        marks_ref[b * OWNERS : (b + 1) * OWNERS, :] = jnp.where(
            target[b : b + 1, :] == sub, 1.0, 0.0
        ).astype(bf16)
    row = lax.broadcasted_iota(jnp.int32, (E, 2 * E), 0)
    col = lax.broadcasted_iota(jnp.int32, (E, 2 * E), 1)
    before = jnp.where(row <= col, 1.0, 0.0).astype(bf16)
    count_ref[...] = jnp.dot(marks_ref[...], before, preferred_element_type=f32)
    run = jnp.zeros((OWNERS, E), f32)
    for b in range(blocks):
        at = slice(b * OWNERS, (b + 1) * OWNERS)
        mark = marks_ref[at, :].astype(f32)
        rank = jnp.sum(mark * (count_ref[at, :E] + run), axis=0, keepdims=True)
        rank_ref[b : b + 1, :] = rank.astype(jnp.int32) - 1
        run = run + count_ref[at, E:]

    list_ref[...] = jnp.zeros(list_ref.shape, f32)
    step = 8
    lane = lax.broadcasted_iota(jnp.int32, (OWNERS, E), 1)
    inner = (((lane >> 2) & 7) * 4 + (lane >> 5)).astype(f32)

    @pl.loop(0, blocks // step)
    def _(c):
        at = pl.ds(pl.multiple_of(c * step, step), step)
        ranks = rank_ref[at, :]
        slots = slot_ref[at, :]
        high = (slots >> 5).astype(f32)
        low = (slots & 31).astype(f32)
        ids = lax.broadcasted_iota(jnp.int32, (CAP, E), 0)
        at_rank, parts = [], []
        for j in range(step):
            one = slice(j, j + 1)
            at_rank.append(jnp.where(ranks[one] == ids, 1.0, 0.0).astype(bf16))
            base = pl.multiple_of(c * (step * OWNERS) + j * OWNERS, OWNERS)
            mark = marks_ref[pl.ds(base, OWNERS), :].astype(f32)
            place = (c * step + j + 1).astype(f32)
            parts.append(
                jnp.concatenate(
                    [mark * high[one], mark * low[one], mark * place, mark * inner], axis=0
                ).astype(bf16)
            )
        list_ref[...] += lax.dot_general(
            jnp.concatenate(parts, axis=1), jnp.concatenate(at_rank, axis=1),
            (((1,), (1,)), ((), ())), preferred_element_type=f32,
        )

    slots = (list_ref[:OWNERS] * 32.0 + list_ref[OWNERS : 2 * OWNERS]).astype(jnp.int32)
    for o in range(OWNERS):
        slots_ref[o] = slots[o : o + 1]
    group = pooled_ref.shape[0]
    place = list_ref[2 * OWNERS : 3 * OWNERS].astype(jnp.int32)
    inner = list_ref[3 * OWNERS :].astype(jnp.int32)
    source = (inner >> 2) * group + (place - 1) * 4 + (inner & 3)
    source = jnp.where(place > 0, source, FEATS * group)
    for q in range(CAP // E):
        from_ref[q * OWNERS : (q + 1) * OWNERS, :] = source[:, q * E : (q + 1) * E]

    preact = jnp.dot(pooled_ref[...], w_ref[...], preferred_element_type=f32)
    sigma = 1.0 / (1.0 + jnp.exp(-preact))
    for c in copies:
        c.wait_recv()
    moved = rbuf[...].reshape(preact.shape)
    grad_pre = (moved.astype(f32) * sigma * (1.0 + preact * (1.0 - sigma))).astype(bf16)
    gw_ref[...] = lax.dot_general(
        pooled_ref[...], grad_pre, (((0,), (0,)), ((), ())), preferred_element_type=f32
    )
    bags_ref[FEATS * group :, :] = jnp.zeros((8, E), f32)
    for f in range(FEATS):
        bags_ref[f * group : (f + 1) * group, :] = (
            lax.dot_general(
                grad_pre, w_ref[f * E : (f + 1) * E, :], (((1,), (1,)), ((), ())),
                preferred_element_type=f32,
            )
            .astype(bf16)
            .astype(f32)
        )
    for c in copies:
        c.wait_send()


def front(grad_out, pooled_rows, weight, owner_rows, slot_rows):
    vmem = pl.BlockSpec(memory_space=pltpu.VMEM)
    samples, towers, cols = grad_out.shape
    group = pooled_rows.shape[0]
    blocks = owner_rows.shape[0]
    return pl.pallas_call(
        front_kernel,
        out_shape=(
            jax.ShapeDtypeStruct((FEATS * group + 8, E), f32),
            jax.ShapeDtypeStruct(weight.shape, f32),
            jax.ShapeDtypeStruct((OWNERS * CAP // E, E), jnp.int32),
            jax.ShapeDtypeStruct((OWNERS, 1, CAP), jnp.int32),
        ),
        in_specs=[vmem] * 5,
        out_specs=(vmem,) * 4,
        scratch_shapes=[
            pltpu.VMEM((towers, samples, cols), bf16),
            pltpu.VMEM((towers, samples, cols), bf16),
            pltpu.VMEM((blocks * OWNERS, E), bf16),
            pltpu.VMEM((blocks * OWNERS, 2 * E), f32),
            pltpu.VMEM((blocks, E), jnp.int32),
            pltpu.VMEM((4 * OWNERS, CAP), f32),
            pltpu.SemaphoreType.DMA((towers,)),
            pltpu.SemaphoreType.DMA((towers,)),
        ],
        compiler_params=pltpu.CompilerParams(collective_id=1, has_side_effects=True),
        name="front",
    )(grad_out, pooled_rows, weight, owner_rows, slot_rows)


def update_kernel(
    rows_ref, lane_ref, grad_ref, table_ref, accum_ref, gw_ref, out_ref, accum_out, gw_out, upd_ref
):
    gw_out[...] = gw_ref[...]
    row_grad = grad_ref[...]
    count = row_grad.shape[0]
    sq_mean = jnp.mean(row_grad * row_grad, axis=1, keepdims=True)
    col = jnp.concatenate(
        [
            jnp.broadcast_to(lane_ref[b : b + 1, :].astype(f32), (E, E)).T
            for b in range(count // E)
        ]
    ).astype(jnp.int32)
    lanes = lax.broadcasted_iota(jnp.int32, (count, E), 1)
    blocks = accum_ref.shape[0]
    high = ((col >> 7) == lanes).astype(f32)[:, :blocks]
    low = ((col & 127) == lanes).astype(f32)
    spread = jnp.dot(high, accum_ref[...], precision=highest, preferred_element_type=f32)
    accum_touched = jnp.sum(spread * low, axis=1, keepdims=True) + sq_mean
    accum_out[...] = accum_ref[...] + lax.dot_general(
        high, low * sq_mean, (((0,), (0,)), ((), ())), precision=highest, preferred_element_type=f32
    )
    upd_ref[...] = learn_rate * row_grad / jnp.sqrt(accum_touched + epsilon)
    out_ref[...] = table_ref[...]

    @pl.loop(0, count // 16)
    def _(i):
        for k in range(16):
            u = i * 16 + k
            r = rows_ref[u]
            out_ref[pl.ds(r, 1), :] = table_ref[pl.ds(r, 1), :] - upd_ref[pl.ds(u, 1), :]


def update(touched, row_grad, table, accum, grad_weight):
    vmem = pl.BlockSpec(memory_space=pltpu.VMEM)
    new_table, new_accum, grad_weight = pl.pallas_call(
        update_kernel,
        out_shape=(
            jax.ShapeDtypeStruct(table.shape, f32),
            jax.ShapeDtypeStruct((accum.shape[0] // E, E), f32),
            jax.ShapeDtypeStruct(grad_weight.shape, f32),
        ),
        in_specs=[pl.BlockSpec(memory_space=pltpu.SMEM), vmem, vmem, vmem, vmem, vmem],
        out_specs=(vmem, vmem, vmem),
        scratch_shapes=[pltpu.VMEM(row_grad.shape, f32)],
        name="row_update",
    )(touched, touched.reshape(-1, E), row_grad, table, accum.reshape(-1, E), grad_weight)
    return new_table, new_accum.reshape(-1), grad_weight


SIDE = 4
HALF = 512
GW_HALF = 16


def reduce_kernel(
    from_ref, bags_ref, slots_ref, gw_ref, out_ref, gw_out, rows_ref, packed_ref,
    pk_recv, sl_recv, gw_recv, s1, r1, s2, r2, own, s3, r3, s4, r4,
    gs1, gr1, gs2, gr2, gown, gs3, gr3, gs4, gr4, send_sem, recv_sem,
):
    me = lax.axis_index("dev")
    core = lax.rem(me, 2)
    chip = me // 2
    x, y = chip // SIDE, lax.rem(chip, SIDE)
    other = 1 - core

    def device(dx, dy):
        return (lax.rem(x + dx, SIDE) * SIDE + lax.rem(y + dy, SIDE)) * 2 + core

    def owner(phase, major, minor):
        dx, dy = (major, minor) if phase == 0 else (minor, major)
        return lax.rem(x + dx, SIDE) * SIDE + lax.rem(y + dy, SIDE)

    def along_major(phase, step):
        return device(step, 0) if phase == 0 else device(0, step)

    def along_minor(phase, step):
        return along_major(1 - phase, step)

    partner = me + 1 - 2 * core
    barrier = pltpu.get_barrier_semaphore()
    for peer in (partner, device(1, 0), device(3, 0), device(0, 1), device(0, 3)):
        pl.semaphore_signal(barrier, inc=1, device_id={"dev": peer}, device_id_type=MESH)
    pl.semaphore_wait(barrier, 5)

    def remote(src, dst, number, peer):
        return pltpu.make_async_remote_copy(
            src_ref=src, dst_ref=dst, send_sem=send_sem.at[number], recv_sem=recv_sem.at[number],
            device_id={"dev": peer}, device_id_type=MESH,
        )

    slot_copy = remote(slots_ref.at[other], sl_recv, 16, partner)
    gw_copy = remote(gw_ref.at[:, other], gw_recv, 17, partner)
    slot_copy.start()
    gw_copy.start()
    pair = {}
    arrived = set()
    part = 64

    def gather(side, o):
        row = (side * (OWNERS // 2) + o) * E

        @pl.loop(0, CAP // part)
        def _(t):
            at = row + (t // 2) * (OWNERS * E) + lax.rem(t, 2) * part
            for k in range(part):
                rows_ref[pl.ds(t * part + k, 1), :] = bags_ref[pl.ds(from_ref[at + k], 1), :]

        packed_ref[side, o] = rows_ref[...].astype(bf16)

    def prepare(keys):
        keys = [key for key in keys if key not in pair]
        for key in keys:
            o = owner(0, *key)
            gather(other, o)
            pair[key] = remote(packed_ref.at[other, o], pk_recv.at[o], len(pair), partner)
            pair[key].start()
        for key in keys:
            gather(core, owner(0, *key))

    def need(phase, major, minors):
        keys = [(major, minor) if phase == 0 else (minor, major) for minor in minors]
        prepare(keys)
        for key in keys:
            if key not in arrived:
                arrived.add(key)
                pair[key].wait_recv()

    def block(phase, major, minor):
        o = owner(phase, major, minor)
        ids = lax.broadcasted_iota(jnp.int32, (HALF, CAP), 0) + phase * HALF
        mine = jnp.where(slots_ref[core, o] == ids, 1.0, 0.0).astype(bf16)
        theirs = jnp.where(sl_recv[o] == ids, 1.0, 0.0).astype(bf16)
        return jnp.dot(mine, packed_ref[core, o], preferred_element_type=f32) + jnp.dot(
            theirs, pk_recv[o], preferred_element_type=f32
        )

    def gw_block(phase, major, minor):
        o = owner(phase, major, minor)
        at = pl.ds(phase * GW_HALF, GW_HALF)
        return gw_ref[o, core, at, :] + gw_recv[o, at, :]

    copies = []

    def copy1(phase, j):
        step = 1 if j < 2 else 3
        return remote(s1.at[phase, j], r1.at[phase, j], 18 + phase * 4 + j, along_major(phase, step))

    def copy2(phase, way, j):
        step = 1 if way == 0 else 3
        return remote(
            s2.at[phase, way, j], r2.at[phase, way, j], 26 + phase * 8 + way * 4 + j,
            along_major(phase, step),
        )

    def small(src, dst, number, peer):
        c = remote(src, dst, number, peer)
        copies.append(c)
        return c

    gw_copy.wait_recv()
    g1 = {}
    for phase in range(2):
        for way in range(2):
            for j in (2 * way, 2 * way + 1):
                gs1[phase, j] = gw_block(phase, 2, j)
            at = pl.ds(2 * way, 2)
            g1[phase, way] = small(
                gs1.at[phase, at], gr1.at[phase, at], 42 + phase * 2 + way,
                along_major(phase, 1 + 2 * way),
            )
            g1[phase, way].start()

    slot_copy.wait_recv()
    first = []
    for phase in range(2):
        need(phase, 2, range(4))
        for j in range(4):
            s1[phase, j] = block(phase, 2, j).astype(bf16)
            c = copy1(phase, j)
            c.start()
            first.append(c)
            copies.append(c)

    sent2 = {}

    def second(phase, way, j, add):
        total = block(phase, 1 + 2 * way, j)
        if add:
            copies_by[phase, j].wait_recv()
            total = total + r1[phase, j].astype(f32)
        s2[phase, way, j] = total.astype(bf16)
        sent2[phase, way, j] = copy2(phase, way, j)
        sent2[phase, way, j].start()

    copies_by = {(phase, j): first[phase * 4 + j] for phase in range(2) for j in range(4)}
    for phase in range(2):
        order = ((0, 2), (1, 1), (0, 3), (1, 0))
        prepare([(1 + 2 * way, j) if phase == 0 else (j, 1 + 2 * way) for way, j in order])
        for way, j in order:
            need(phase, 1 + 2 * way, (j,))
            second(phase, way, j, False)
    for phase in range(2):
        order = ((1, 2), (0, 1), (1, 3), (0, 0))
        prepare([(1 + 2 * way, j) if phase == 0 else (j, 1 + 2 * way) for way, j in order])
        for way, j in order:
            need(phase, 1 + 2 * way, (j,))
            second(phase, way, j, True)
    g2 = {}
    for phase in range(2):
        for way in range(2):
            g1[phase, way].wait_recv()
            for j in range(4):
                total = gw_block(phase, 1 + 2 * way, j)
                if j // 2 == way:
                    total = total + gr1[phase, j]
                gs2[phase, way, j] = total
            g2[phase, way] = small(
                gs2.at[phase, way], gr2.at[phase, way], 46 + phase * 2 + way,
                along_major(phase, 1 + 2 * way),
            )
            g2[phase, way].start()
    for phase in range(2):
        need(phase, 0, range(4))
        for j in range(4):
            own[phase, j] = block(phase, 0, j)
            gown[phase, j] = gw_block(phase, 0, j)

    def gathered(phase, j):
        for way in range(2):
            sent2[phase, way, j].wait_recv()
        return own[phase, j] + r2[phase, 0, j].astype(f32) + r2[phase, 1, j].astype(f32)

    sent3, sent4, g3, g4 = {}, {}, {}, {}
    quarter = HALF // 2
    for phase in range(2):
        total = gathered(phase, 2)
        for way in range(2):
            s3[phase, way] = total[way * quarter : (way + 1) * quarter].astype(bf16)
            sent3[phase, way] = small(
                s3.at[phase, way], r3.at[phase, way], 50 + phase * 2 + way,
                along_minor(phase, 1 + 2 * way),
            )
            sent3[phase, way].start()
    for phase in range(2):
        for way in range(2):
            g2[phase, way].wait_recv()
        for j in range(4):
            gown[phase, j] = gown[phase, j] + gr2[phase, 0, j] + gr2[phase, 1, j]
        for way in range(2):
            gs3[phase, way] = gown[phase, 2, 8 * way : 8 * way + 8]
            g3[phase, way] = small(
                gs3.at[phase, way], gr3.at[phase, way], 54 + phase * 2 + way,
                along_minor(phase, 1 + 2 * way),
            )
            g3[phase, way].start()
    for phase in range(2):
        for way in range(2):
            total = gathered(phase, 1 + 2 * way)
            sent3[phase, way].wait_recv()
            for part in range(2):
                at = slice(part * quarter, (part + 1) * quarter)
                piece = total[at]
                if part == way:
                    piece = piece + r3[phase, way].astype(f32)
                s4[phase, way, at] = piece.astype(bf16)
            sent4[phase, way] = small(
                s4.at[phase, way], r4.at[phase, way], 58 + phase * 2 + way,
                along_minor(phase, 1 + 2 * way),
            )
            sent4[phase, way].start()
            g3[phase, way].wait_recv()
            for part in range(2):
                at = slice(8 * part, 8 * part + 8)
                piece = gown[phase, 1 + 2 * way, at]
                if part == way:
                    piece = piece + gr3[phase, way]
                gs4[phase, way, at] = piece
            g4[phase, way] = small(
                gs4.at[phase, way], gr4.at[phase, way], 62 + phase * 2 + way,
                along_minor(phase, 1 + 2 * way),
            )
            g4[phase, way].start()
    for phase in range(2):
        own[phase, 0] = gathered(phase, 0)
    for phase in range(2):
        for way in range(2):
            sent4[phase, way].wait_recv()
            g4[phase, way].wait_recv()
        out_ref[pl.ds(phase * HALF, HALF), :] = (
            own[phase, 0] + r4[phase, 0].astype(f32) + r4[phase, 1].astype(f32)
        )
        gw_out[pl.ds(phase * GW_HALF, GW_HALF), :] = gown[phase, 0] + gr4[phase, 0] + gr4[phase, 1]
    for c in [slot_copy, gw_copy, *pair.values(), *copies, *sent2.values()]:
        c.wait_send()


def reduce_rows(source, bags, slots, grad_weight):
    vmem = pl.BlockSpec(memory_space=pltpu.VMEM)
    cols = grad_weight.shape[-1]
    halves = (HALF, E)
    small = (GW_HALF, cols)
    return pl.pallas_call(
        reduce_kernel,
        out_shape=(
            jax.ShapeDtypeStruct((2 * HALF, E), f32),
            jax.ShapeDtypeStruct((2 * GW_HALF, cols), f32),
        ),
        in_specs=[pl.BlockSpec(memory_space=pltpu.SMEM), vmem, vmem, vmem],
        out_specs=(vmem, vmem),
        scratch_shapes=[
            pltpu.VMEM((CAP, E), f32),
            pltpu.VMEM((2, 16, CAP, E), bf16),
            pltpu.VMEM((16, CAP, E), bf16),
            pltpu.VMEM((16, 1, CAP), jnp.int32),
            pltpu.VMEM((16, 2 * GW_HALF, cols), f32),
            pltpu.VMEM((2, 4, *halves), bf16),
            pltpu.VMEM((2, 4, *halves), bf16),
            pltpu.VMEM((2, 2, 4, *halves), bf16),
            pltpu.VMEM((2, 2, 4, *halves), bf16),
            pltpu.VMEM((2, 4, *halves), f32),
            pltpu.VMEM((2, 2, HALF // 2, E), bf16),
            pltpu.VMEM((2, 2, HALF // 2, E), bf16),
            pltpu.VMEM((2, 2, *halves), bf16),
            pltpu.VMEM((2, 2, *halves), bf16),
            pltpu.VMEM((2, 4, *small), f32),
            pltpu.VMEM((2, 4, *small), f32),
            pltpu.VMEM((2, 2, 4, *small), f32),
            pltpu.VMEM((2, 2, 4, *small), f32),
            pltpu.VMEM((2, 4, *small), f32),
            pltpu.VMEM((2, 2, GW_HALF // 2, cols), f32),
            pltpu.VMEM((2, 2, GW_HALF // 2, cols), f32),
            pltpu.VMEM((2, 2, *small), f32),
            pltpu.VMEM((2, 2, *small), f32),
            pltpu.SemaphoreType.DMA((66,)),
            pltpu.SemaphoreType.DMA((66,)),
        ],
        compiler_params=pltpu.CompilerParams(collective_id=0, has_side_effects=True),
        name="reduce_rows",
    )(source, bags, slots, grad_weight)


def shards(grad_out, pooled, compress_w, owner_ids, slot_ids, touched, table, accum):
    chips = OWNERS // 2
    bags, grad_weight, source, slots = front(
        grad_out,
        pooled[0, 0],
        compress_w[0],
        owner_ids.reshape(-1, E),
        slot_ids.reshape(-1, E),
    )
    row_grad, grad_weight = reduce_rows(
        source.reshape(-1),
        bags,
        slots.reshape(2, chips, 1, CAP),
        grad_weight.reshape(chips, 2, -1, grad_weight.shape[1]),
    )
    new_table, new_accum, grad_weight = update(
        touched[0, 0], row_grad, table[0], accum[0], grad_weight
    )
    return (grad_weight[None], new_table[None], new_accum[None])


def solution(mesh):
    return jax.shard_map(
        shards,
        mesh=mesh,
        in_specs=(
            P(("tower", "dev"), None, None),
            P("tower", "dev", None, None),
            P("tower", None, None),
            P("tower", "dev", None, None),
            P("tower", "dev", None),
            P("tower", "dev", None),
            P("tower", "dev", None),
            P("tower", "dev"),
        ),
        out_specs=(P("tower", "dev", None), P("tower", "dev", None), P("tower", "dev")),
        check_vma=False,
    )
```
